512 devices in a mesh: region: 64 (over z, x), split: 8 (over y, core).
Axes of the slice: x: 4, y: 4, z: 16, core: 2. Of those that a mesh axis runs over, the one named last changes fastest.
Arguments:
- vectors: float32 [294912, 256], P(('region', 'split'))
- hessian: bfloat16 [1536, 12, 192, 192], P(('region', 'split')), may hold values from -0.125 to 0.125
- block_cols: int32 [1536, 12], P(('region', 'split')), may hold values from 0 to 35, as said below
- live_blocks: int32 [1536], P(('region', 'split')), may hold values from 6 to 12, as said below
- halo_lists: int32 [64, 2, 6], P('region'), may hold values from 0 to 23, as said below
- bounds: float32 [2], replicated, as said below
Outputs:
- basis: float32 [294912, 256], P(('region', 'split'))
- projected: float32 [256, 256], replicated
The draws below stay inside these ranges and needn't reach their ends.
Inputs may be any that keep to these rules, and one draw needn't show every extreme that they name: `block_cols`: in each row the entries are distinct and entry 0 is the row's own block within its region; values below 24 name blocks of the row's region, 24 + j the j-th block received from the lower region, 30 + j the j-th from the upper region. `live_blocks`: the first block row of every region has all 12 blocks intact. `halo_lists`: each list holds distinct block indices within the region. bounds[0] < 0 < bounds[1].
All inputs are finite; a program needn't handle non-finite values.
Results may differ from the reference program's by a relative error of at most 0.0005.
The reference program's roundings to bfloat16 on the way count: a program that leaves them out, or rounds other values in their place, can miss the bound.
Values may be sent and summed in bfloat16 or wider, within the bound.
A program may use at most 64 MiB of HBM per device.

```python
import math
import jax
import jax.numpy as jnp
from jax import lax

BS = 192
M = 256
NNZ = 12
HB = 6
REGION_BLOCKS = 24
BLOCK_ROWS = 1536
DOFS = 294912
CANDS = 36
N_REGION = 64


def draw_vectors(key, part):
    first_key, second_key = jax.random.split(key, 2)
    base = jax.random.normal(first_key, (DOFS, M), jnp.float32)
    rising = 1.0 + 2.0 * jnp.arange(DOFS, dtype=jnp.float32) / DOFS
    column_scale = jnp.exp(jax.random.uniform(second_key, (1, M), jnp.float32, 0.0, math.log(10.0)))
    return base * rising[:, None] * column_scale


def draw_block_cols(key, part):
    scores = jax.random.randint(jax.random.fold_in(key, 11), (BLOCK_ROWS, CANDS), 0, 65536)
    scores = scores * CANDS + jnp.arange(CANDS, dtype=jnp.int32)[None, :]
    cand_index = jnp.arange(CANDS, dtype=jnp.int32)[None, :]
    own_block = jnp.arange(BLOCK_ROWS, dtype=jnp.int32) % REGION_BLOCKS
    first_row = (own_block == 0)[:, None]
    scores = jnp.where(first_row & (cand_index == CANDS - 1), 2 ** 30 - 1, scores)
    scores = jnp.where(cand_index == own_block[:, None], 2 ** 30, scores)
    return lax.top_k(scores, NNZ)[1].astype(jnp.int32)


def draw_live_blocks(key, part):
    counts = jax.random.randint(jax.random.fold_in(key, 12), (BLOCK_ROWS,), NNZ // 2, NNZ + 1)
    return counts.at[::REGION_BLOCKS].set(NNZ).astype(jnp.int32)


def draw_halo_lists(key, part):
    scores = jax.random.randint(jax.random.fold_in(key, 13), (N_REGION, 2, REGION_BLOCKS), 0, 65536)
    scores = scores * REGION_BLOCKS + jnp.arange(REGION_BLOCKS, dtype=jnp.int32)
    scores = scores.at[0, 0, REGION_BLOCKS - 1].set(-1)
    scores = scores.at[0, 1, 0].set(-1)
    order = jnp.argsort(scores, axis=-1, stable=True)
    return order[:, :, :HB].astype(jnp.int32)


def draw_bounds(key, part):
    first_key, second_key = jax.random.split(jax.random.fold_in(key, 14))
    lower_end = jax.random.uniform(first_key, (1,), jnp.float32, -0.4, -0.05)
    upper_end = jax.random.uniform(second_key, (1,), jnp.float32, 0.9, 1.4)
    return jnp.concatenate([lower_end, upper_end], 0)


def level_of(stream_key, dims, pieces, smallest, largest):
    factor_of = 1.0
    for axis_at, parts in pieces:
        draws = jax.random.uniform(jax.random.fold_in(jax.random.fold_in(stream_key, 6), axis_at), (parts,), jnp.float32, smallest / len(pieces), largest / len(pieces))
        factor_of = factor_of * jnp.repeat(jnp.exp(draws), dims[axis_at] // parts).reshape((-1,) + (1,) * (len(dims) - 1 - axis_at))
    return factor_of


def centred(stream_key, dims, scale, limit, pieces=(), kind=jnp.bfloat16):
    result = jax.random.normal(stream_key, dims, jnp.float32) * scale
    if len(pieces) > 0:
        result = level_of(stream_key, dims, pieces, -0.22, 0.18) * result
    return jnp.clip(result, min=-limit, max=limit).astype(kind)


def setup_inputs(seed: int = 0) -> dict:
    key_of = jax.random.split(jax.random.key(seed), 7)
    return {
        "vectors": draw_vectors(jax.random.fold_in(key_of[6], 71), 0),
        "hessian": centred(key_of[1], (BLOCK_ROWS, NNZ, BS, BS), (NNZ * BS) ** -0.5, 0.125, ((0, 512),)),
        "block_cols": draw_block_cols(jax.random.fold_in(key_of[6], 71), 0),
        "live_blocks": draw_live_blocks(jax.random.fold_in(key_of[6], 71), 0),
        "halo_lists": draw_halo_lists(jax.random.fold_in(key_of[6], 71), 0),
        "bounds": draw_bounds(jax.random.fold_in(key_of[6], 71), 0),
    }


def apply_blocks(operand, hessian, block_cols, live_blocks, halo_lists):
    regions = operand.reshape(N_REGION, REGION_BLOCKS, BS, M)
    hess_regions = hessian.reshape(N_REGION, REGION_BLOCKS, NNZ, BS, BS)
    cols_regions = block_cols.reshape(N_REGION, REGION_BLOCKS, NNZ)
    live_regions = live_blocks.reshape(N_REGION, REGION_BLOCKS)

    def per_region(region_index):
        own_blocks = regions[region_index]
        lower_index = (region_index - 1) % N_REGION
        upper_index = (region_index + 1) % N_REGION
        from_lower = regions[lower_index][halo_lists[lower_index, 1]]
        from_upper = regions[upper_index][halo_lists[upper_index, 0]]
        candidates = jnp.concatenate([own_blocks, from_lower, from_upper], 0)
        picked = candidates[cols_regions[region_index]].astype(jnp.float32)
        used_mask = jnp.arange(NNZ)[None, :] < live_regions[region_index][:, None]
        picked = jnp.where(used_mask[:, :, None, None], picked, jnp.zeros((), jnp.float32))
        return jnp.einsum('rkij,rkjm->rim', hess_regions[region_index].astype(jnp.float32), picked)
    product = lax.map(per_region, jnp.arange(N_REGION, dtype=jnp.int32))
    return product.reshape(DOFS, M)

def reference(vectors, hessian, block_cols, live_blocks, halo_lists, bounds):
    centre = 0.5 * (bounds[0] + bounds[1])
    half_width = 0.5 * (bounds[1] - bounds[0])
    first = apply_blocks(vectors.astype(jnp.bfloat16), hessian, block_cols, live_blocks, halo_lists)
    filtered_one = (first - centre * vectors) / half_width
    second = apply_blocks(filtered_one.astype(jnp.bfloat16), hessian, block_cols, live_blocks, halo_lists)
    filtered_two = 2.0 * (second - centre * filtered_one) / half_width - vectors
    image = apply_blocks(filtered_two.astype(jnp.bfloat16), hessian, block_cols, live_blocks, halo_lists)
    gram = jnp.dot(filtered_two.T, filtered_two, precision=lax.Precision.HIGHEST) / DOFS
    cross = jnp.dot(filtered_two.T, image, precision=lax.Precision.HIGHEST) / DOFS
    lower = jnp.linalg.cholesky(gram)
    basis = jax.scipy.linalg.solve_triangular(lower, filtered_two.T, lower=True).T
    partial_left = jax.scipy.linalg.solve_triangular(lower, cross, lower=True)
    projected = jax.scipy.linalg.solve_triangular(lower, partial_left.T, lower=True).T
    return (basis, projected)
```

```python
import functools

import jax
import jax.numpy as jnp
from jax import lax
from jax.experimental import pallas as pl
from jax.experimental.pallas import tpu as pltpu
from jax.sharding import PartitionSpec as P

MESH = pl.DeviceIdType.MESH
HIGH = lax.Precision.HIGHEST
X = 4
PIECES = 3
AHEAD = 2
PANEL = 32


def dot_high(a, b, dims=(((1,), (0,)), ((), ()))):
    return lax.dot_general(a, b, dims, precision=HIGH, preferred_element_type=jnp.float32)


def factor_inverse(block):
    size = block.shape[0]
    row_id = lax.broadcasted_iota(jnp.int32, (size, size), 0)
    eye = jnp.where(row_id == lax.broadcasted_iota(jnp.int32, (size, size), 1), 1.0, 0.0)
    work = jnp.concatenate([block, eye.astype(jnp.float32)], axis=1)
    rows = lax.broadcasted_iota(jnp.int32, work.shape, 0)
    for j in range(size):
        scale = lax.rsqrt(work[j : j + 1, j : j + 1])
        row = work[j : j + 1, :] * scale
        column = work[:, j : j + 1] * scale
        work = jnp.where(rows > j, work - column * row, jnp.where(rows == j, row, work))
    return work[:, size:]


def kernel(dims, vec_hbm, hes_hbm, cols, live, lists, bounds, basis, proj, *scratch):
    n_region, n_split, rb, bs, m, nnz, hb, total_rows = dims
    n_z, n_y = n_region // X, n_split // 2
    blocks = rb * n_split
    piece = bs // PIECES
    half_piece = piece // 2
    plane = X * n_split
    chunk = m // plane
    share = hb // 2

    it = iter(scratch)
    vec, hes, hcat, picks = next(it), next(it), next(it), next(it)
    reg = [[next(it) for _ in range(PIECES)] for _ in range(3)]
    hal = [[next(it) for _ in range(PIECES)] for _ in range(3)]
    stg = [[next(it) for _ in range(PIECES)] for _ in range(3)]
    one, two, two_t, img = next(it), next(it), next(it), next(it)
    part = [next(it) for _ in range(2)]
    rs = [next(it) for _ in range(2)]
    zb = [next(it) for _ in range(2)]
    full = [next(it) for _ in range(2)]
    aug = next(it)
    in_sem, g_send, g_recv, h_send, h_recv, a_send, a_recv = (next(it) for _ in range(7))

    r = lax.axis_index("region")
    s = lax.axis_index("split")
    z, x = r // X, r % X
    y, c = s // 2, s % 2
    mate = y * 2 + 1 - c
    up_s = ((y + 1) % n_y) * 2 + c
    down_s = ((y + n_y - 1) % n_y) * 2 + c
    far_s = ((y + 2) % n_y) * 2 + c
    upper = (r + 1) % n_region
    lower = (r + n_region - 1) % n_region
    w = x * n_split + s

    copy_v = pltpu.make_async_copy(vec_hbm, vec, in_sem.at[0])
    copy_h = pltpu.make_async_copy(hes_hbm, hes, in_sem.at[1])
    copy_v.start()
    copy_h.start()

    barrier = pltpu.get_barrier_semaphore()

    def signal(region, split):
        pl.semaphore_signal(barrier, inc=1, device_id=(region, split), device_id_type=MESH)

    def greet_plane(o, carry):
        p = (w + o) % plane
        signal(z * X + p // n_split, p % n_split)
        return carry

    def greet_line(o, carry):
        signal(((z + o) % n_z) * X + x, s)
        return carry

    lax.fori_loop(1, n_z, greet_line, 0)
    lax.fori_loop(1, plane, greet_plane, 0)
    signal(upper, s)
    signal(lower, s)

    def put_own(a, value):
        for q in range(PIECES):
            for b in range(rb):
                reg[a][q][s * rb + b] = value[b * bs + q * piece : b * bs + (q + 1) * piece, :].astype(
                    jnp.bfloat16
                )

    pending = []

    def remote(src, dst, ssem, rsem, region, split):
        copy = pltpu.make_async_remote_copy(
            src_ref=src,
            dst_ref=dst,
            send_sem=ssem,
            recv_sem=rsem,
            device_id=(region, split),
            device_id_type=MESH,
        )
        copy.start()
        pending.append(copy)
        return copy

    def gather_copy(a, q, kind, owner, rows, split):
        view = reg[a][q].at[pl.ds(owner * rb, rb), pl.ds(rows[0], rows[1] - rows[0]), :]
        at = (a * PIECES + q) * 9 + kind
        return remote(view, view, g_send.at[at], g_recv.at[at], r, split)

    whole, low, high = (0, piece), (0, half_piece), (half_piece, piece)

    def wait_gather(a, q, kind, owner, rows):
        view = reg[a][q].at[pl.ds(owner * rb, rb), pl.ds(rows[0], rows[1] - rows[0]), :]
        at = (a * PIECES + q) * 9 + kind
        pltpu.make_async_remote_copy(
            src_ref=view,
            dst_ref=view,
            send_sem=g_send.at[at],
            recv_sem=g_recv.at[at],
            device_id=(r, mate),
            device_id_type=MESH,
        ).wait_recv()

    def send_own(a, q):
        gather_copy(a, q, 0, s, whole, up_s)
        gather_copy(a, q, 1, s, whole, down_s)
        gather_copy(a, q, 4, s, whole, mate)

    def relay(a, q):
        wait_gather(a, q, 0, down_s, whole)
        gather_copy(a, q, 2, down_s, low, up_s)
        wait_gather(a, q, 1, up_s, whole)
        gather_copy(a, q, 3, up_s, high, down_s)
        gather_copy(a, q, 5, down_s, whole, mate)
        gather_copy(a, q, 6, up_s, whole, mate)

    def finish_gather(a, q):
        wait_gather(a, q, 2, far_s, low)
        gather_copy(a, q, 7, far_s, low, mate)
        wait_gather(a, q, 3, far_s, high)
        gather_copy(a, q, 8, far_s, high, mate)
        other = 1 - 2 * c
        wait_gather(a, q, 4, s + other, whole)
        wait_gather(a, q, 5, down_s + other, whole)
        wait_gather(a, q, 6, up_s + other, whole)
        wait_gather(a, q, 7, far_s + other, low)
        wait_gather(a, q, 8, far_s + other, high)

    def halo_view(a, q, d, core):
        return hal[a][q].at[pl.ds((1 - d) * hb + core * share, share)]

    def halo_copy(a, q, d, kind, src, dst, region, split):
        at = ((a * PIECES + q) * 2 + d) * 2 + kind
        return remote(src, dst, h_send.at[at], h_recv.at[at], region, split)

    def wait_halo(a, q, d, kind, core):
        view = halo_view(a, q, d, core)
        at = ((a * PIECES + q) * 2 + d) * 2 + kind
        pltpu.make_async_remote_copy(
            src_ref=view,
            dst_ref=view,
            send_sem=h_send.at[at],
            recv_sem=h_recv.at[at],
            device_id=(r, mate),
            device_id_type=MESH,
        ).wait_recv()

    def send_halo(a, q):
        for d in range(2):
            for j in range(share):
                stg[a][q][d, j] = reg[a][q][lists[0, d, c * share + j]]
            halo_copy(a, q, d, 0, stg[a][q].at[d], halo_view(a, q, d, c), (lower, upper)[d], s)

    def pass_halo(a, q):
        for d in (1, 0):
            wait_halo(a, q, d, 0, c)
            view = halo_view(a, q, d, c)
            halo_copy(a, q, d, 1, view, view, r, mate)

    def finish_halo(a, q):
        for d in (1, 0):
            wait_halo(a, q, d, 1, 1 - c)

    def start_apply(a):
        for q in range(min(AHEAD, PIECES)):
            send_own(a, q)

    def exchange(a, between=None):
        for q in range(PIECES):
            relay(a, q)
            if q + AHEAD < PIECES:
                send_own(a, q + AHEAD)
            if q >= 1:
                finish_gather(a, q - 1)
                send_halo(a, q - 1)
            if q >= 2:
                pass_halo(a, q - 2)
        finish_gather(a, PIECES - 1)
        send_halo(a, PIECES - 1)
        if between is not None:
            between()
        for q in range(max(PIECES - 2, 0), PIECES):
            pass_halo(a, q)
        for q in range(PIECES):
            finish_halo(a, q)

    def multiply(a, i):
        for k in range(nnz):
            col = cols[i, k]
            alive = k < live[i]
            inside = col < blocks
            near = jnp.where(inside, col, 0)
            away = jnp.where(alive, jnp.where(inside, 0, col - blocks), 2 * hb)
            use = jnp.logical_and(alive, inside)
            for q in range(PIECES):
                picks[pl.ds(k * bs + q * piece, piece), :] = jnp.where(
                    use, reg[a][q][near], hal[a][q][away]
                )
        return jnp.dot(hcat[i], picks[...], preferred_element_type=jnp.float32)

    def reduce_send(t):
        def body(o, carry):
            p = (w + o) % plane
            pltpu.make_async_remote_copy(
                src_ref=part[t].at[p],
                dst_ref=rs[t].at[o - 1],
                send_sem=a_send.at[t * 3],
                recv_sem=a_recv.at[t * 3],
                device_id=(z * X + p // n_split, p % n_split),
                device_id_type=MESH,
            ).start()
            return carry

        lax.fori_loop(1, plane, body, 0)

    def bulk(ref, at):
        return pltpu.make_async_remote_copy(
            src_ref=ref,
            dst_ref=ref,
            send_sem=a_send.at[at],
            recv_sem=a_recv.at[at],
            device_id=(r, mate),
            device_id_type=MESH,
        )

    def reduce_line(t):
        bulk(rs[t], t * 3).wait_recv()
        value = part[t][w]
        for o in range(plane - 1):
            value = value + rs[t][o]
        zb[t][z] = value

        def body(o, carry):
            pltpu.make_async_remote_copy(
                src_ref=zb[t].at[z],
                dst_ref=zb[t].at[z],
                send_sem=a_send.at[t * 3 + 1],
                recv_sem=a_recv.at[t * 3 + 1],
                device_id=(((z + o) % n_z) * X + x, s),
                device_id_type=MESH,
            ).start()
            return carry

        lax.fori_loop(1, n_z, body, 0)

    def spread(t):
        bulk(zb[t].at[pl.ds(0, n_z - 1)], t * 3 + 1).wait_recv()
        value = zb[t][0]
        for o in range(1, n_z):
            value = value + zb[t][o]
        full[t][w] = value / total_rows

        def body(o, carry):
            p = (w + o) % plane
            pltpu.make_async_remote_copy(
                src_ref=full[t].at[w],
                dst_ref=full[t].at[w],
                send_sem=a_send.at[t * 3 + 2],
                recv_sem=a_recv.at[t * 3 + 2],
                device_id=(z * X + p // n_split, p % n_split),
                device_id_type=MESH,
            ).start()
            return carry

        lax.fori_loop(1, plane, body, 0)

    def collected(t):
        bulk(full[t].at[pl.ds(0, plane - 1)], t * 3 + 2).wait_recv()
        return full[t][...].reshape(m, m)

    def drain(t):
        bulk(rs[t], t * 3).wait_send()
        bulk(zb[t].at[pl.ds(0, n_z - 1)], t * 3 + 1).wait_send()
        bulk(full[t].at[pl.ds(0, plane - 1)], t * 3 + 2).wait_send()

    for a in range(3):
        for q in range(PIECES):
            hal[a][q][2 * hb] = jnp.zeros((piece, m), jnp.bfloat16)
    copy_v.wait()
    put_own(0, vec[...])
    pl.semaphore_wait(barrier, plane - 1 + n_z - 1 + 2)
    start_apply(0)
    copy_h.wait()

    def join(i, carry):
        for k in range(0, nnz, 2):
            hcat[i, :, k * bs : (k + 2) * bs] = jnp.concatenate([hes[i, k], hes[i, k + 1]], axis=1)
        return carry

    lax.fori_loop(0, rb, join, 0)
    exchange(0)
    centre = 0.5 * (bounds[0] + bounds[1])
    half = 0.5 * (bounds[1] - bounds[0])

    def step_one(i, carry):
        at = pl.ds(pl.multiple_of(i * bs, bs), bs)
        one[at, :] = (multiply(0, i) - centre * vec[at, :]) / half
        return carry

    def step_two(i, carry):
        at = pl.ds(pl.multiple_of(i * bs, bs), bs)
        two[at, :] = 2.0 * (multiply(1, i) - centre * one[at, :]) / half - vec[at, :]
        return carry

    def step_image(i, carry):
        at = pl.ds(pl.multiple_of(i * bs, bs), bs)
        img[at, :] = multiply(2, i)
        return carry

    lax.fori_loop(0, rb, step_one, 0)
    put_own(1, one[...])
    start_apply(1)
    exchange(1)
    lax.fori_loop(0, rb, step_two, 0)
    put_own(2, two[...])
    start_apply(2)
    two_t[...] = two[...].T
    part[0][...] = dot_high(two_t[...], two[...]).reshape(plane, chunk, m)
    reduce_send(0)
    exchange(2, lambda: reduce_line(0))
    lax.fori_loop(0, rb, step_image, 0)
    part[1][...] = dot_high(two_t[...], img[...]).reshape(plane, chunk, m)
    reduce_send(1)
    spread(0)

    row_id = lax.broadcasted_iota(jnp.int32, (m, m), 0)
    col_id = lax.broadcasted_iota(jnp.int32, (m, m), 1)
    aug[:, m:] = jnp.where(row_id == col_id, 1.0, 0.0).astype(jnp.float32)
    aug[:, :m] = collected(0)

    def panel(p):
        at = p * PANEL
        end = at + PANEL
        inverse = factor_inverse(aug[at:end, at:end])
        rows = dot_high(inverse, aug[at:end, :])
        aug[at:end, :] = rows
        if end < m:
            left = rows[:, end:m].T
            aug[end:, :] = aug[end:, :] - dot_high(left, rows)

    panels = m // PANEL
    for p in range(panels // 2):
        panel(p)
    reduce_line(1)
    for p in range(panels // 2, panels):
        panel(p)
    spread(1)
    inverse = aug[:, m:]
    nt = (((1,), (1,)), ((), ()))
    basis[...] = dot_high(two[...], inverse, nt)
    cross = collected(1)
    proj[...] = dot_high(dot_high(inverse, cross), inverse, nt)
    for copy in pending:
        copy.wait_send()
    drain(0)
    drain(1)


def local(sizes, vectors, hessian, block_cols, live_blocks, halo_lists, bounds):
    n_region, n_split = sizes
    rb, nnz, bs, _ = hessian.shape
    m = vectors.shape[1]
    hb = halo_lists.shape[2]
    rows = vectors.shape[0]
    dims = (n_region, n_split, rb, bs, m, nnz, hb, float(rows * n_region * n_split))
    piece = bs // PIECES
    blocks = rb * n_split
    plane = X * n_split
    chunk = m // plane
    n_z = n_region // X
    f32, bf16 = jnp.float32, jnp.bfloat16
    scratch = [
        pltpu.VMEM((rows, m), f32),
        pltpu.VMEM((rb, nnz, bs, bs), bf16),
        pltpu.VMEM((rb, bs, nnz * bs), bf16),
        pltpu.VMEM((nnz * bs, m), bf16),
    ]
    scratch += [pltpu.VMEM((blocks, piece, m), bf16) for _ in range(3 * PIECES)]
    scratch += [pltpu.VMEM((2 * hb + 1, piece, m), bf16) for _ in range(3 * PIECES)]
    scratch += [pltpu.VMEM((2, hb // 2, piece, m), bf16) for _ in range(3 * PIECES)]
    scratch += [
        pltpu.VMEM((rows, m), f32),
        pltpu.VMEM((rows, m), f32),
        pltpu.VMEM((m, rows), f32),
        pltpu.VMEM((rows, m), f32),
    ]
    scratch += [pltpu.VMEM((plane, chunk, m), f32)] * 2
    scratch += [pltpu.VMEM((plane - 1, chunk, m), f32)] * 2
    scratch += [pltpu.VMEM((n_z, chunk, m), f32)] * 2
    scratch += [pltpu.VMEM((plane, chunk, m), f32)] * 2
    scratch += [pltpu.VMEM((m, 2 * m), f32)]
    dma = pltpu.SemaphoreType.DMA
    scratch += [
        dma((2,)),
        dma((27 * PIECES,)),
        dma((27 * PIECES,)),
        dma((12 * PIECES,)),
        dma((12 * PIECES,)),
        dma((6,)),
        dma((6,)),
    ]
    smem = pl.BlockSpec(memory_space=pltpu.SMEM)
    hbm = pl.BlockSpec(memory_space=pl.ANY)
    vmem = pl.BlockSpec(memory_space=pltpu.VMEM)
    return pl.pallas_call(
        functools.partial(kernel, dims),
        out_shape=(jax.ShapeDtypeStruct((rows, m), f32), jax.ShapeDtypeStruct((m, m), f32)),
        in_specs=[hbm, hbm, smem, smem, smem, smem],
        out_specs=(vmem, vmem),
        scratch_shapes=scratch,
        compiler_params=pltpu.CompilerParams(
            collective_id=0, has_side_effects=True, vmem_limit_bytes=58 * 2**20
        ),
    )(vectors, hessian, block_cols, live_blocks, halo_lists, bounds)


def solution(mesh):
    placed = (
        P(("region", "split"), None),
        P(("region", "split"), None, None, None),
        P(("region", "split"), None),
        P(("region", "split")),
        P("region", None, None),
        P(),
    )
    return jax.shard_map(
        functools.partial(local, (mesh.shape["region"], mesh.shape["split"])),
        mesh=mesh,
        in_specs=placed,
        out_specs=(P(("region", "split"), None), P()),
        check_vma=False,
    )
```

```python
import functools

import jax
import jax.numpy as jnp
from jax import lax
from jax.experimental import pallas as pl
from jax.experimental.pallas import tpu as pltpu
from jax.sharding import PartitionSpec as P

MESH = pl.DeviceIdType.MESH
HIGH = lax.Precision.HIGHEST
X = 4
PIECES = 3
AHEAD = 2
PANEL = 64
GROUP = 16
RS_AT, LINE_AT = ("relay", 2), ("pass", 0)
SPREAD_AT = 3


def dot_high(a, b, dims=(((1,), (0,)), ((), ()))):
    return lax.dot_general(a, b, dims, precision=HIGH, preferred_element_type=jnp.float32)


def factor_inverse(block):
    size = block.shape[0]
    row_id = lax.broadcasted_iota(jnp.int32, (size, size), 0)
    same = row_id == lax.broadcasted_iota(jnp.int32, (size, size), 1)
    work = jnp.concatenate([block, jnp.where(same, 1.0, 0.0).astype(jnp.float32)], axis=1)
    rows = lax.broadcasted_iota(jnp.int32, work.shape, 0)
    for first in range(0, size, GROUP):
        wide = [
            jnp.broadcast_to(work[:, first + t : first + t + 1], work.shape) for t in range(GROUP)
        ]
        for t in range(GROUP):
            j = first + t
            over = 1.0 / wide[t][j : j + 1, :]
            below = jnp.where(rows > j, wide[t], 0.0)
            work = work - below * (work[j : j + 1, :] * over)
            for u in range(t + 1, GROUP):
                wide[u] = wide[u] - below * (wide[u][j : j + 1, :] * over)
    pivots = jnp.sum(jnp.where(same, work[:, :size], 0.0), axis=1, keepdims=True)
    return work[:, size:] * lax.rsqrt(pivots)


def kernel(dims, vec_hbm, hes_hbm, cols, live, lists, bounds, basis, proj, *scratch):
    n_region, n_split, rb, bs, m, nnz, hb, total_rows = dims
    n_z, n_y = n_region // X, n_split // 2
    blocks = rb * n_split
    piece = bs // PIECES
    half_piece = piece // 2
    plane = X * n_split
    chunk = m // plane
    share = hb // 2

    it = iter(scratch)
    vec, hes, hcat, picks = next(it), next(it), next(it), next(it)
    reg = [[next(it) for _ in range(PIECES)] for _ in range(3)]
    hal = [[next(it) for _ in range(PIECES)] for _ in range(3)]
    stg = [[next(it) for _ in range(PIECES)] for _ in range(3)]
    one, two, two_t, img = next(it), next(it), next(it), next(it)
    part = [next(it) for _ in range(2)]
    rs = [next(it) for _ in range(2)]
    zb = [next(it) for _ in range(2)]
    full = [next(it) for _ in range(2)]
    aug = next(it)
    in_sem, g_send, g_recv, h_send, h_recv, a_send, a_recv, token = (next(it) for _ in range(8))

    r = lax.axis_index("region")
    s = lax.axis_index("split")
    z, x = r // X, r % X
    y, c = s // 2, s % 2
    mate = y * 2 + 1 - c
    up_s = ((y + 1) % n_y) * 2 + c
    down_s = ((y + n_y - 1) % n_y) * 2 + c
    far_s = ((y + 2) % n_y) * 2 + c
    upper = (r + 1) % n_region
    lower = (r + n_region - 1) % n_region
    w = x * n_split + s

    copy_v = pltpu.make_async_copy(vec_hbm, vec, in_sem.at[0])
    copy_h = pltpu.make_async_copy(hes_hbm, hes, in_sem.at[1])
    copy_v.start()
    copy_h.start()

    barrier = pltpu.get_barrier_semaphore()

    def signal(region, split):
        pl.semaphore_signal(barrier, inc=1, device_id=(region, split), device_id_type=MESH)

    def greet_split(o, carry):
        signal(r, (s + o) % n_split)
        return carry

    ring = (
        (z * X + (x + 1) % X, z * X + (x + X - 1) % X),
        (((z + 1) % n_z) * X + x, ((z + n_z - 1) % n_z) * X + x),
    )
    for region in (upper, lower) + ring[1] + ring[0]:
        signal(region, s)
    lax.fori_loop(1, n_split, greet_split, 0)

    rounds = (X // 2, max(n_z // 2 - 1, 0))
    ticks = []

    def pass_tokens(k):
        for axis in range(2):
            for side in range(2):
                if k <= rounds[axis]:
                    if k > 1:
                        pl.semaphore_wait(token.at[axis, k - 2, side], 1)
        for axis in range(2):
            for side in range(2):
                if k <= rounds[axis]:
                    pl.semaphore_signal(
                        token.at[axis, k - 1, side],
                        inc=1,
                        device_id=(ring[axis][side], s),
                        device_id_type=MESH,
                    )

    def tick():
        if len(ticks) < max(rounds):
            ticks.append(0)
            pass_tokens(len(ticks))

    def all_ticks():
        while len(ticks) < max(rounds):
            tick()
        for axis in range(2):
            for side in range(2):
                if rounds[axis] > 0:
                    pl.semaphore_wait(token.at[axis, rounds[axis] - 1, side], 1)

    def put_own(a, value):
        for q in range(PIECES):
            for b in range(rb):
                reg[a][q][s * rb + b] = value[b * bs + q * piece : b * bs + (q + 1) * piece, :].astype(
                    jnp.bfloat16
                )

    pending = []

    def remote(src, dst, ssem, rsem, region, split):
        copy = pltpu.make_async_remote_copy(
            src_ref=src,
            dst_ref=dst,
            send_sem=ssem,
            recv_sem=rsem,
            device_id=(region, split),
            device_id_type=MESH,
        )
        copy.start()
        pending.append(copy)
        return copy

    def gather_copy(a, q, kind, owner, rows, split):
        view = reg[a][q].at[pl.ds(owner * rb, rb), pl.ds(rows[0], rows[1] - rows[0]), :]
        at = (a * PIECES + q) * 9 + kind
        return remote(view, view, g_send.at[at], g_recv.at[at], r, split)

    whole, low, high = (0, piece), (0, half_piece), (half_piece, piece)

    def wait_gather(a, q, kind, owner, rows):
        view = reg[a][q].at[pl.ds(owner * rb, rb), pl.ds(rows[0], rows[1] - rows[0]), :]
        at = (a * PIECES + q) * 9 + kind
        pltpu.make_async_remote_copy(
            src_ref=view,
            dst_ref=view,
            send_sem=g_send.at[at],
            recv_sem=g_recv.at[at],
            device_id=(r, mate),
            device_id_type=MESH,
        ).wait_recv()

    def send_own(a, q):
        gather_copy(a, q, 0, s, whole, up_s)
        gather_copy(a, q, 1, s, whole, down_s)
        gather_copy(a, q, 4, s, whole, mate)

    def relay(a, q):
        wait_gather(a, q, 0, down_s, whole)
        gather_copy(a, q, 2, down_s, low, up_s)
        wait_gather(a, q, 1, up_s, whole)
        gather_copy(a, q, 3, up_s, high, down_s)
        gather_copy(a, q, 5, down_s, whole, mate)
        gather_copy(a, q, 6, up_s, whole, mate)

    def finish_gather(a, q):
        wait_gather(a, q, 2, far_s, low)
        gather_copy(a, q, 7, far_s, low, mate)
        wait_gather(a, q, 3, far_s, high)
        gather_copy(a, q, 8, far_s, high, mate)
        other = 1 - 2 * c
        wait_gather(a, q, 4, s + other, whole)
        wait_gather(a, q, 5, down_s + other, whole)
        wait_gather(a, q, 6, up_s + other, whole)
        wait_gather(a, q, 7, far_s + other, low)
        wait_gather(a, q, 8, far_s + other, high)

    def halo_view(a, q, d, core):
        return hal[a][q].at[pl.ds((1 - d) * hb + core * share, share)]

    def halo_copy(a, q, d, kind, src, dst, region, split):
        at = ((a * PIECES + q) * 2 + d) * 2 + kind
        return remote(src, dst, h_send.at[at], h_recv.at[at], region, split)

    def wait_halo(a, q, d, kind, core):
        view = halo_view(a, q, d, core)
        at = ((a * PIECES + q) * 2 + d) * 2 + kind
        pltpu.make_async_remote_copy(
            src_ref=view,
            dst_ref=view,
            send_sem=h_send.at[at],
            recv_sem=h_recv.at[at],
            device_id=(r, mate),
            device_id_type=MESH,
        ).wait_recv()

    def send_halo(a, q):
        for d in range(2):
            for j in range(share):
                stg[a][q][d, j] = reg[a][q][lists[0, d, c * share + j]]
            halo_copy(a, q, d, 0, stg[a][q].at[d], halo_view(a, q, d, c), (lower, upper)[d], s)

    def pass_halo(a, q):
        for d in (1, 0):
            wait_halo(a, q, d, 0, c)
            view = halo_view(a, q, d, c)
            halo_copy(a, q, d, 1, view, view, r, mate)

    def finish_halo(a, q):
        for d in (1, 0):
            wait_halo(a, q, d, 1, 1 - c)

    def start_apply(a):
        for q in range(min(AHEAD, PIECES)):
            send_own(a, q)

    def exchange(a, hooks=()):
        hooks = dict(hooks)

        def reached(name, q):
            if (name, q) in hooks:
                hooks[name, q]()

        for q in range(PIECES):
            relay(a, q)
            if q + AHEAD < PIECES:
                send_own(a, q + AHEAD)
            tick()
            reached("relay", q)
            if q >= 1:
                finish_gather(a, q - 1)
                send_halo(a, q - 1)
                reached("select", q - 1)
        finish_gather(a, PIECES - 1)
        send_halo(a, PIECES - 1)
        reached("select", PIECES - 1)
        tick()
        for q in range(PIECES):
            pass_halo(a, q)
            reached("pass", q)
        for q in range(PIECES):
            finish_halo(a, q)

    def multiply(a, i):
        for k in range(nnz):
            col = cols[i, k]
            alive = k < live[i]
            inside = col < blocks
            near = jnp.where(inside, col, 0)
            away = jnp.where(alive, jnp.where(inside, 0, col - blocks), 2 * hb)
            use = jnp.logical_and(alive, inside)
            for q in range(PIECES):
                picks[pl.ds(k * bs + q * piece, piece), :] = jnp.where(
                    use, reg[a][q][near], hal[a][q][away]
                )
        return jnp.dot(hcat[i], picks[...], preferred_element_type=jnp.float32)

    def reduce_send(t):
        def body(o, carry):
            p = (w + o) % plane
            pltpu.make_async_remote_copy(
                src_ref=part[t].at[p],
                dst_ref=rs[t].at[o - 1],
                send_sem=a_send.at[t * 3],
                recv_sem=a_recv.at[t * 3],
                device_id=(z * X + p // n_split, p % n_split),
                device_id_type=MESH,
            ).start()
            return carry

        lax.fori_loop(plane // 2, plane, body, 0)
        lax.fori_loop(1, plane // 2, body, 0)

    def bulk(ref, at):
        return pltpu.make_async_remote_copy(
            src_ref=ref,
            dst_ref=ref,
            send_sem=a_send.at[at],
            recv_sem=a_recv.at[at],
            device_id=(r, mate),
            device_id_type=MESH,
        )

    def reduce_line(t):
        bulk(rs[t], t * 3).wait_recv()
        value = part[t][w]
        for o in range(plane - 1):
            value = value + rs[t][o]
        zb[t][z] = value

        def body(o, carry):
            pltpu.make_async_remote_copy(
                src_ref=zb[t].at[z],
                dst_ref=zb[t].at[z],
                send_sem=a_send.at[t * 3 + 1],
                recv_sem=a_recv.at[t * 3 + 1],
                device_id=(((z + n_z // 2 + (1 - 2 * (o % 2)) * ((o + 1) // 2)) % n_z) * X + x, s),
                device_id_type=MESH,
            ).start()
            return carry

        lax.fori_loop(0, n_z - 1, body, 0)

    def spread(t):
        bulk(zb[t].at[pl.ds(0, n_z - 1)], t * 3 + 1).wait_recv()
        value = zb[t][0]
        for o in range(1, n_z):
            value = value + zb[t][o]
        full[t][w] = value / total_rows

        def body(o, carry):
            p = (w + o) % plane
            pltpu.make_async_remote_copy(
                src_ref=full[t].at[w],
                dst_ref=full[t].at[w],
                send_sem=a_send.at[t * 3 + 2],
                recv_sem=a_recv.at[t * 3 + 2],
                device_id=(z * X + p // n_split, p % n_split),
                device_id_type=MESH,
            ).start()
            return carry

        lax.fori_loop(plane // 2, plane, body, 0)
        lax.fori_loop(1, plane // 2, body, 0)

    def collected(t):
        bulk(full[t].at[pl.ds(0, plane - 1)], t * 3 + 2).wait_recv()
        return full[t][...].reshape(m, m)

    def drain(t):
        bulk(rs[t], t * 3).wait_send()
        bulk(zb[t].at[pl.ds(0, n_z - 1)], t * 3 + 1).wait_send()
        bulk(full[t].at[pl.ds(0, plane - 1)], t * 3 + 2).wait_send()

    for a in range(3):
        for q in range(PIECES):
            hal[a][q][2 * hb] = jnp.zeros((piece, m), jnp.bfloat16)
    copy_v.wait()
    put_own(0, vec[...])
    pl.semaphore_wait(barrier, n_split - 1 + 6)
    start_apply(0)
    copy_h.wait()

    def join(i, carry):
        for k in range(0, nnz, 2):
            hcat[i, :, k * bs : (k + 2) * bs] = jnp.concatenate([hes[i, k], hes[i, k + 1]], axis=1)
        return carry

    lax.fori_loop(0, rb, join, 0)
    exchange(0)
    centre = 0.5 * (bounds[0] + bounds[1])
    half = 0.5 * (bounds[1] - bounds[0])

    def step_one(i, carry):
        at = pl.ds(pl.multiple_of(i * bs, bs), bs)
        one[at, :] = (multiply(0, i) - centre * vec[at, :]) / half
        return carry

    def step_two(i, carry):
        at = pl.ds(pl.multiple_of(i * bs, bs), bs)
        two[at, :] = 2.0 * (multiply(1, i) - centre * one[at, :]) / half - vec[at, :]
        return carry

    def step_image(i, carry):
        at = pl.ds(pl.multiple_of(i * bs, bs), bs)
        img[at, :] = multiply(2, i)
        return carry

    lax.fori_loop(0, rb, step_one, 0)
    put_own(1, one[...])
    start_apply(1)
    exchange(1)
    lax.fori_loop(0, rb, step_two, 0)
    put_own(2, two[...])
    start_apply(2)
    two_t[...] = two[...].T
    part[0][...] = dot_high(two_t[...], two[...]).reshape(plane, chunk, m)
    all_ticks()
    exchange(
        2,
        {
            RS_AT: lambda: reduce_send(0),
            LINE_AT: lambda: reduce_line(0),
        },
    )
    lax.fori_loop(0, rb, step_image, 0)
    part[1][...] = dot_high(two_t[...], img[...]).reshape(plane, chunk, m)
    reduce_send(1)
    spread(0)
    reduce_line(1)

    row_id = lax.broadcasted_iota(jnp.int32, (m, m), 0)
    col_id = lax.broadcasted_iota(jnp.int32, (m, m), 1)
    aug[:, m:] = jnp.where(row_id == col_id, 1.0, 0.0).astype(jnp.float32)
    aug[:, :m] = collected(0)

    def panel(p):
        at = p * PANEL
        end = at + PANEL
        inverse = factor_inverse(aug[at:end, at:end])
        rows = dot_high(inverse, aug[at:end, :])
        aug[at:end, :] = rows
        if end < m:
            left = rows[:, end:m].T
            aug[end:, :] = aug[end:, :] - dot_high(left, rows)

    panels = m // PANEL
    for p in range(panels):
        panel(p)
        if p == SPREAD_AT:
            spread(1)
    inverse = aug[:, m:]
    nt = (((1,), (1,)), ((), ()))
    basis[...] = dot_high(two[...], inverse, nt)
    cross = collected(1)
    proj[...] = dot_high(dot_high(inverse, cross), inverse, nt)
    for copy in pending:
        copy.wait_send()
    drain(0)
    drain(1)


def local(sizes, vectors, hessian, block_cols, live_blocks, halo_lists, bounds):
    n_region, n_split = sizes
    rb, nnz, bs, _ = hessian.shape
    m = vectors.shape[1]
    hb = halo_lists.shape[2]
    rows = vectors.shape[0]
    dims = (n_region, n_split, rb, bs, m, nnz, hb, float(rows * n_region * n_split))
    piece = bs // PIECES
    blocks = rb * n_split
    plane = X * n_split
    chunk = m // plane
    n_z = n_region // X
    f32, bf16 = jnp.float32, jnp.bfloat16
    scratch = [
        pltpu.VMEM((rows, m), f32),
        pltpu.VMEM((rb, nnz, bs, bs), bf16),
        pltpu.VMEM((rb, bs, nnz * bs), bf16),
        pltpu.VMEM((nnz * bs, m), bf16),
    ]
    scratch += [pltpu.VMEM((blocks, piece, m), bf16) for _ in range(3 * PIECES)]
    scratch += [pltpu.VMEM((2 * hb + 1, piece, m), bf16) for _ in range(3 * PIECES)]
    scratch += [pltpu.VMEM((2, hb // 2, piece, m), bf16) for _ in range(3 * PIECES)]
    scratch += [
        pltpu.VMEM((rows, m), f32),
        pltpu.VMEM((rows, m), f32),
        pltpu.VMEM((m, rows), f32),
        pltpu.VMEM((rows, m), f32),
    ]
    scratch += [pltpu.VMEM((plane, chunk, m), f32)] * 2
    scratch += [pltpu.VMEM((plane - 1, chunk, m), f32)] * 2
    scratch += [pltpu.VMEM((n_z, chunk, m), f32)] * 2
    scratch += [pltpu.VMEM((plane, chunk, m), f32)] * 2
    scratch += [pltpu.VMEM((m, 2 * m), f32)]
    dma = pltpu.SemaphoreType.DMA
    scratch += [
        dma((2,)),
        dma((27 * PIECES,)),
        dma((27 * PIECES,)),
        dma((12 * PIECES,)),
        dma((12 * PIECES,)),
        dma((6,)),
        dma((6,)),
        pltpu.SemaphoreType.REGULAR((2, 8, 2)),
    ]
    smem = pl.BlockSpec(memory_space=pltpu.SMEM)
    hbm = pl.BlockSpec(memory_space=pl.ANY)
    vmem = pl.BlockSpec(memory_space=pltpu.VMEM)
    return pl.pallas_call(
        functools.partial(kernel, dims),
        out_shape=(jax.ShapeDtypeStruct((rows, m), f32), jax.ShapeDtypeStruct((m, m), f32)),
        in_specs=[hbm, hbm, smem, smem, smem, smem],
        out_specs=(vmem, vmem),
        scratch_shapes=scratch,
        compiler_params=pltpu.CompilerParams(
            collective_id=0, has_side_effects=True, vmem_limit_bytes=58 * 2**20
        ),
    )(vectors, hessian, block_cols, live_blocks, halo_lists, bounds)


def solution(mesh):
    placed = (
        P(("region", "split"), None),
        P(("region", "split"), None, None, None),
        P(("region", "split"), None),
        P(("region", "split")),
        P("region", None, None),
        P(),
    )
    return jax.shard_map(
        functools.partial(local, (mesh.shape["region"], mesh.shape["split"])),
        mesh=mesh,
        in_specs=placed,
        out_specs=(P(("region", "split"), None), P()),
        check_vma=False,
    )
```

```python
import functools

import jax
import jax.numpy as jnp
from jax import lax
from jax.experimental import pallas as pl
from jax.experimental.pallas import tpu as pltpu
from jax.sharding import PartitionSpec as P

MESH = pl.DeviceIdType.MESH
HIGH = lax.Precision.HIGHEST
TRANSPOSED = (((1,), (1,)), ((), ()))
X = 4
PIECES = 3
AHEAD = 2
PANEL = 64
GROUP = 16
RS_AT, LINE_AT = ("select", 0), ("pass", 0)
SPREAD_AT = 2


def dot_high(a, b, dims=(((1,), (0,)), ((), ()))):
    return lax.dot_general(a, b, dims, precision=HIGH, preferred_element_type=jnp.float32)


def factor_inverse(block):
    size = block.shape[0]
    row_id = lax.broadcasted_iota(jnp.int32, (size, size), 0)
    same = row_id == lax.broadcasted_iota(jnp.int32, (size, size), 1)
    work = jnp.concatenate([block, jnp.where(same, 1.0, 0.0).astype(jnp.float32)], axis=1)
    rows = lax.broadcasted_iota(jnp.int32, work.shape, 0)
    for first in range(0, size, GROUP):
        wide = [
            jnp.broadcast_to(work[:, first + t : first + t + 1], work.shape) for t in range(GROUP)
        ]
        for t in range(GROUP):
            j = first + t
            over = 1.0 / wide[t][j : j + 1, :]
            below = jnp.where(rows > j, wide[t], 0.0)
            work = work - below * (work[j : j + 1, :] * over)
            for u in range(t + 1, GROUP):
                wide[u] = wide[u] - below * (wide[u][j : j + 1, :] * over)
    pivots = jnp.sum(jnp.where(same, work[:, :size], 0.0), axis=1, keepdims=True)
    return work[:, size:] * lax.rsqrt(pivots)


def kernel(dims, vec_hbm, hes_hbm, cols, live, lists, bounds, basis, inv_out, cross_out, *scratch):
    n_region, n_split, rb, bs, m, nnz, hb, total_rows = dims
    n_z, n_y = n_region // X, n_split // 2
    blocks = rb * n_split
    piece = bs // PIECES
    half_piece = piece // 2
    plane = X * n_split
    chunk = m // plane
    share = hb // 2

    it = iter(scratch)
    vec, hes, hcat, picks = next(it), next(it), next(it), next(it)
    reg = [[next(it) for _ in range(PIECES)] for _ in range(3)]
    hal = [[next(it) for _ in range(PIECES)] for _ in range(3)]
    stg = [[next(it) for _ in range(PIECES)] for _ in range(3)]
    one, two, two_t, img = next(it), next(it), next(it), next(it)
    part = [next(it) for _ in range(2)]
    rs = [next(it) for _ in range(2)]
    zb = [next(it) for _ in range(2)]
    gram_full, own_chunk = next(it), [next(it) for _ in range(2)]
    full = [gram_full, cross_out]
    aug = next(it)
    in_sem, g_send, g_recv, h_send, h_recv, a_send, a_recv, token, out_sem = (
        next(it) for _ in range(9)
    )

    r = lax.axis_index("region")
    s = lax.axis_index("split")
    z, x = r // X, r % X
    y, c = s // 2, s % 2
    mate = y * 2 + 1 - c
    up_s = ((y + 1) % n_y) * 2 + c
    down_s = ((y + n_y - 1) % n_y) * 2 + c
    far_s = ((y + 2) % n_y) * 2 + c
    upper = (r + 1) % n_region
    lower = (r + n_region - 1) % n_region
    w = x * n_split + s

    copy_v = pltpu.make_async_copy(vec_hbm, vec, in_sem.at[0])
    copy_h = pltpu.make_async_copy(hes_hbm, hes, in_sem.at[1])
    copy_v.start()
    copy_h.start()

    barrier = pltpu.get_barrier_semaphore()

    def signal(region, split):
        pl.semaphore_signal(barrier, inc=1, device_id=(region, split), device_id_type=MESH)

    def greet_split(o, carry):
        signal(r, (s + o) % n_split)
        return carry

    ring = (
        (z * X + (x + 1) % X, z * X + (x + X - 1) % X),
        (((z + 1) % n_z) * X + x, ((z + n_z - 1) % n_z) * X + x),
    )
    for region in (upper, lower) + ring[1] + ring[0]:
        signal(region, s)
    lax.fori_loop(1, n_split, greet_split, 0)

    rounds = (X // 2, max(n_z // 2 - 1, 0))
    ticks = []

    def pass_tokens(k):
        for axis in range(2):
            for side in range(2):
                if k <= rounds[axis]:
                    if k > 1:
                        pl.semaphore_wait(token.at[axis, k - 2, side], 1)
        for axis in range(2):
            for side in range(2):
                if k <= rounds[axis]:
                    pl.semaphore_signal(
                        token.at[axis, k - 1, side],
                        inc=1,
                        device_id=(ring[axis][side], s),
                        device_id_type=MESH,
                    )

    def tick():
        if len(ticks) < max(rounds):
            ticks.append(0)
            pass_tokens(len(ticks))

    def all_ticks():
        while len(ticks) < max(rounds):
            tick()
        for axis in range(2):
            for side in range(2):
                if rounds[axis] > 0:
                    pl.semaphore_wait(token.at[axis, rounds[axis] - 1, side], 1)

    def put_own(a, value):
        for q in range(PIECES):
            for b in range(rb):
                reg[a][q][s * rb + b] = value[b * bs + q * piece : b * bs + (q + 1) * piece, :].astype(
                    jnp.bfloat16
                )

    pending = []

    def remote(src, dst, ssem, rsem, region, split):
        copy = pltpu.make_async_remote_copy(
            src_ref=src,
            dst_ref=dst,
            send_sem=ssem,
            recv_sem=rsem,
            device_id=(region, split),
            device_id_type=MESH,
        )
        copy.start()
        pending.append(copy)
        return copy

    def gather_copy(a, q, kind, owner, rows, split):
        view = reg[a][q].at[pl.ds(owner * rb, rb), pl.ds(rows[0], rows[1] - rows[0]), :]
        at = (a * PIECES + q) * 9 + kind
        return remote(view, view, g_send.at[at], g_recv.at[at], r, split)

    whole, low, high = (0, piece), (0, half_piece), (half_piece, piece)

    def wait_gather(a, q, kind, owner, rows):
        view = reg[a][q].at[pl.ds(owner * rb, rb), pl.ds(rows[0], rows[1] - rows[0]), :]
        at = (a * PIECES + q) * 9 + kind
        pltpu.make_async_remote_copy(
            src_ref=view,
            dst_ref=view,
            send_sem=g_send.at[at],
            recv_sem=g_recv.at[at],
            device_id=(r, mate),
            device_id_type=MESH,
        ).wait_recv()

    def send_own(a, q):
        gather_copy(a, q, 0, s, whole, up_s)
        gather_copy(a, q, 1, s, whole, down_s)
        gather_copy(a, q, 4, s, whole, mate)

    def relay(a, q):
        wait_gather(a, q, 0, down_s, whole)
        gather_copy(a, q, 2, down_s, low, up_s)
        wait_gather(a, q, 1, up_s, whole)
        gather_copy(a, q, 3, up_s, high, down_s)
        gather_copy(a, q, 5, down_s, whole, mate)
        gather_copy(a, q, 6, up_s, whole, mate)

    def finish_gather(a, q):
        wait_gather(a, q, 2, far_s, low)
        gather_copy(a, q, 7, far_s, low, mate)
        wait_gather(a, q, 3, far_s, high)
        gather_copy(a, q, 8, far_s, high, mate)
        other = 1 - 2 * c
        wait_gather(a, q, 4, s + other, whole)
        wait_gather(a, q, 5, down_s + other, whole)
        wait_gather(a, q, 6, up_s + other, whole)
        wait_gather(a, q, 7, far_s + other, low)
        wait_gather(a, q, 8, far_s + other, high)

    def halo_view(a, q, d, core):
        return hal[a][q].at[pl.ds((1 - d) * hb + core * share, share)]

    def halo_copy(a, q, d, kind, src, dst, region, split):
        at = ((a * PIECES + q) * 2 + d) * 2 + kind
        return remote(src, dst, h_send.at[at], h_recv.at[at], region, split)

    def wait_halo(a, q, d, kind, core):
        view = halo_view(a, q, d, core)
        at = ((a * PIECES + q) * 2 + d) * 2 + kind
        pltpu.make_async_remote_copy(
            src_ref=view,
            dst_ref=view,
            send_sem=h_send.at[at],
            recv_sem=h_recv.at[at],
            device_id=(r, mate),
            device_id_type=MESH,
        ).wait_recv()

    def send_halo(a, q):
        for d in range(2):
            for j in range(share):
                stg[a][q][d, j] = reg[a][q][lists[0, d, c * share + j]]
            halo_copy(a, q, d, 0, stg[a][q].at[d], halo_view(a, q, d, c), (lower, upper)[d], s)

    def pass_halo(a, q):
        for d in (1, 0):
            wait_halo(a, q, d, 0, c)
            view = halo_view(a, q, d, c)
            halo_copy(a, q, d, 1, view, view, r, mate)

    def finish_halo(a, q):
        for d in (1, 0):
            wait_halo(a, q, d, 1, 1 - c)

    def start_apply(a):
        for q in range(min(AHEAD, PIECES)):
            send_own(a, q)

    def exchange(a, hooks=()):
        hooks = dict(hooks)

        def reached(name, q):
            if (name, q) in hooks:
                hooks[name, q]()

        for q in range(PIECES):
            relay(a, q)
            if q + AHEAD < PIECES:
                send_own(a, q + AHEAD)
            if a == 1:
                tick()
            reached("relay", q)
            if q >= 1:
                finish_gather(a, q - 1)
                send_halo(a, q - 1)
                reached("select", q - 1)
        finish_gather(a, PIECES - 1)
        send_halo(a, PIECES - 1)
        reached("select", PIECES - 1)
        tick()
        for q in range(PIECES):
            pass_halo(a, q)
            if a == 0:
                tick()
            reached("pass", q)
        for q in range(PIECES):
            finish_halo(a, q)

    def multiply(a, i):
        for k in range(nnz):
            col = cols[i, k]
            alive = k < live[i]
            inside = col < blocks
            near = jnp.where(inside, col, 0)
            away = jnp.where(alive, jnp.where(inside, 0, col - blocks), 2 * hb)
            use = jnp.logical_and(alive, inside)
            for q in range(PIECES):
                picks[pl.ds(k * bs + q * piece, piece), :] = jnp.where(
                    use, reg[a][q][near], hal[a][q][away]
                )
        return jnp.dot(hcat[i], picks[...], preferred_element_type=jnp.float32)

    def reduce_send(t):
        def body(o, carry):
            p = (w + o) % plane
            pltpu.make_async_remote_copy(
                src_ref=part[t].at[p],
                dst_ref=rs[t].at[o - 1],
                send_sem=a_send.at[t * 3],
                recv_sem=a_recv.at[t * 3],
                device_id=(z * X + p // n_split, p % n_split),
                device_id_type=MESH,
            ).start()
            return carry

        lax.fori_loop(plane // 2, plane, body, 0)
        lax.fori_loop(1, plane // 2, body, 0)

    def bulk(ref, at):
        return pltpu.make_async_remote_copy(
            src_ref=ref,
            dst_ref=ref,
            send_sem=a_send.at[at],
            recv_sem=a_recv.at[at],
            device_id=(r, mate),
            device_id_type=MESH,
        )

    def reduce_line(t):
        bulk(rs[t], t * 3).wait_recv()
        value = part[t][w]
        for o in range(plane - 1):
            value = value + rs[t][o]
        zb[t][z] = value

        def body(o, carry):
            pltpu.make_async_remote_copy(
                src_ref=zb[t].at[z],
                dst_ref=zb[t].at[z],
                send_sem=a_send.at[t * 3 + 1],
                recv_sem=a_recv.at[t * 3 + 1],
                device_id=(((z + n_z // 2 + (1 - 2 * (o % 2)) * ((o + 1) // 2)) % n_z) * X + x, s),
                device_id_type=MESH,
            ).start()
            return carry

        lax.fori_loop(0, n_z - 1, body, 0)

    def spread(t):
        bulk(zb[t].at[pl.ds(0, n_z - 1)], t * 3 + 1).wait_recv()
        value = zb[t][0]
        for o in range(1, n_z):
            value = value + zb[t][o]
        own_chunk[t][...] = value / total_rows
        pltpu.make_async_copy(own_chunk[t], full[t].at[w], out_sem.at[t]).start()

        def body(o, carry):
            p = (w + o) % plane
            pltpu.make_async_remote_copy(
                src_ref=own_chunk[t],
                dst_ref=full[t].at[w],
                send_sem=a_send.at[t * 3 + 2],
                recv_sem=a_recv.at[t * 3 + 2],
                device_id=(z * X + p // n_split, p % n_split),
                device_id_type=MESH,
            ).start()
            return carry

        lax.fori_loop(plane // 2, plane, body, 0)
        lax.fori_loop(1, plane // 2, body, 0)

    def collected(t):
        bulk(full[t].at[pl.ds(0, plane - 1)], t * 3 + 2).wait_recv()
        pltpu.make_async_copy(own_chunk[t], full[t].at[w], out_sem.at[t]).wait()

    def drain(t):
        bulk(rs[t], t * 3).wait_send()
        bulk(zb[t].at[pl.ds(0, n_z - 1)], t * 3 + 1).wait_send()
        bulk(full[t].at[pl.ds(0, plane - 1)], t * 3 + 2).wait_send()

    for a in range(3):
        for q in range(PIECES):
            hal[a][q][2 * hb] = jnp.zeros((piece, m), jnp.bfloat16)
    copy_v.wait()
    put_own(0, vec[...])
    pl.semaphore_wait(barrier, n_split - 1 + 6)
    start_apply(0)
    copy_h.wait()

    def join(i, carry):
        for k in range(0, nnz, 2):
            hcat[i, :, k * bs : (k + 2) * bs] = jnp.concatenate([hes[i, k], hes[i, k + 1]], axis=1)
        return carry

    lax.fori_loop(0, rb, join, 0)
    exchange(0)
    centre = 0.5 * (bounds[0] + bounds[1])
    half = 0.5 * (bounds[1] - bounds[0])

    def step_one(i, carry):
        at = pl.ds(pl.multiple_of(i * bs, bs), bs)
        one[at, :] = (multiply(0, i) - centre * vec[at, :]) / half
        return carry

    def step_two(i, carry):
        at = pl.ds(pl.multiple_of(i * bs, bs), bs)
        two[at, :] = 2.0 * (multiply(1, i) - centre * one[at, :]) / half - vec[at, :]
        return carry

    def step_image(i, carry):
        at = pl.ds(pl.multiple_of(i * bs, bs), bs)
        img[at, :] = multiply(2, i)
        return carry

    lax.fori_loop(0, rb, step_one, 0)
    put_own(1, one[...])
    start_apply(1)
    exchange(1)
    lax.fori_loop(0, rb, step_two, 0)
    put_own(2, two[...])
    start_apply(2)
    two_t[...] = two[...].T
    part[0][...] = dot_high(two_t[...], two[...]).reshape(plane, chunk, m)
    all_ticks()
    exchange(
        2,
        {
            RS_AT: lambda: reduce_send(0),
            LINE_AT: lambda: reduce_line(0),
        },
    )
    lax.fori_loop(0, rb, step_image, 0)
    part[1][...] = dot_high(two_t[...], img[...]).reshape(plane, chunk, m)
    reduce_send(1)
    spread(0)
    reduce_line(1)

    row_id = lax.broadcasted_iota(jnp.int32, (m, m), 0)
    col_id = lax.broadcasted_iota(jnp.int32, (m, m), 1)
    aug[:, m:] = jnp.where(row_id == col_id, 1.0, 0.0).astype(jnp.float32)
    collected(0)
    aug[:, :m] = gram_full[...].reshape(m, m)

    def panel(p):
        at = p * PANEL
        end = at + PANEL
        inverse = factor_inverse(aug[at:end, at:end])
        rows = dot_high(inverse, aug[at:end, :])
        aug[at:end, :] = rows
        if end < m:
            left = rows[:, end:m].T
            aug[end:, :] = aug[end:, :] - dot_high(left, rows)

    panels = m // PANEL
    for p in range(panels):
        panel(p)
        if p == SPREAD_AT:
            spread(1)
    copy_inv = pltpu.make_async_copy(aug.at[:, pl.ds(m, m)], inv_out, out_sem.at[2])
    copy_inv.start()
    one[...] = dot_high(two[...], aug[:, m:], TRANSPOSED)
    copy_basis = pltpu.make_async_copy(one, basis, out_sem.at[3])
    copy_basis.start()
    for copy in pending:
        copy.wait_send()
    drain(0)
    drain(1)
    copy_inv.wait()
    copy_basis.wait()
    collected(1)


def finish(basis_in, inv_in, cross_in, basis_out, proj_out, basis, inv, cross, proj, sem):
    inputs = [
        pltpu.make_async_copy(a, b, sem.at[i])
        for i, (a, b) in enumerate(((inv_in, inv), (cross_in, cross), (basis_in, basis)))
    ]
    for copy in inputs:
        copy.start()
    inputs[0].wait()
    inputs[1].wait()
    proj[...] = dot_high(dot_high(inv[...], cross[...]), inv[...], TRANSPOSED)
    copy_proj = pltpu.make_async_copy(proj, proj_out, sem.at[3])
    copy_proj.start()
    inputs[2].wait()
    copy_basis = pltpu.make_async_copy(basis, basis_out, sem.at[4])
    copy_basis.start()
    copy_proj.wait()
    copy_basis.wait()


def local(sizes, vectors, hessian, block_cols, live_blocks, halo_lists, bounds):
    n_region, n_split = sizes
    rb, nnz, bs, _ = hessian.shape
    m = vectors.shape[1]
    hb = halo_lists.shape[2]
    rows = vectors.shape[0]
    dims = (n_region, n_split, rb, bs, m, nnz, hb, float(rows * n_region * n_split))
    piece = bs // PIECES
    blocks = rb * n_split
    plane = X * n_split
    chunk = m // plane
    n_z = n_region // X
    f32, bf16 = jnp.float32, jnp.bfloat16
    scratch = [
        pltpu.VMEM((rows, m), f32),
        pltpu.VMEM((rb, nnz, bs, bs), bf16),
        pltpu.VMEM((rb, bs, nnz * bs), bf16),
        pltpu.VMEM((nnz * bs, m), bf16),
    ]
    scratch += [pltpu.VMEM((blocks, piece, m), bf16) for _ in range(3 * PIECES)]
    scratch += [pltpu.VMEM((2 * hb + 1, piece, m), bf16) for _ in range(3 * PIECES)]
    scratch += [pltpu.VMEM((2, hb // 2, piece, m), bf16) for _ in range(3 * PIECES)]
    scratch += [
        pltpu.VMEM((rows, m), f32),
        pltpu.VMEM((rows, m), f32),
        pltpu.VMEM((m, rows), f32),
        pltpu.VMEM((rows, m), f32),
    ]
    scratch += [pltpu.VMEM((plane, chunk, m), f32)] * 2
    scratch += [pltpu.VMEM((plane - 1, chunk, m), f32)] * 2
    scratch += [pltpu.VMEM((n_z, chunk, m), f32)] * 2
    scratch += [pltpu.VMEM((plane, chunk, m), f32)]
    scratch += [pltpu.VMEM((chunk, m), f32)] * 2
    scratch += [pltpu.VMEM((m, 2 * m), f32)]
    dma = pltpu.SemaphoreType.DMA
    scratch += [
        dma((2,)),
        dma((27 * PIECES,)),
        dma((27 * PIECES,)),
        dma((12 * PIECES,)),
        dma((12 * PIECES,)),
        dma((6,)),
        dma((6,)),
        pltpu.SemaphoreType.REGULAR((2, 8, 2)),
        dma((4,)),
    ]
    smem = pl.BlockSpec(memory_space=pltpu.SMEM)
    hbm = pl.BlockSpec(memory_space=pl.ANY)
    basis, inverse, cross = pl.pallas_call(
        functools.partial(kernel, dims),
        out_shape=(
            jax.ShapeDtypeStruct((rows, m), f32),
            jax.ShapeDtypeStruct((m, m), f32),
            jax.ShapeDtypeStruct((plane, chunk, m), f32),
        ),
        in_specs=[hbm, hbm, smem, smem, smem, smem],
        out_specs=(hbm, hbm, hbm),
        scratch_shapes=scratch,
        compiler_params=pltpu.CompilerParams(
            collective_id=0, has_side_effects=True, vmem_limit_bytes=58 * 2**20
        ),
    )(vectors, hessian, block_cols, live_blocks, halo_lists, bounds)
    return pl.pallas_call(
        finish,
        out_shape=(jax.ShapeDtypeStruct((rows, m), f32), jax.ShapeDtypeStruct((m, m), f32)),
        in_specs=[hbm, hbm, hbm],
        out_specs=(hbm, hbm),
        scratch_shapes=[
            pltpu.VMEM((rows, m), f32),
            pltpu.VMEM((m, m), f32),
            pltpu.VMEM((m, m), f32),
            pltpu.VMEM((m, m), f32),
            dma((5,)),
        ],
        compiler_params=pltpu.CompilerParams(vmem_limit_bytes=58 * 2**20),
    )(basis, inverse, cross.reshape(m, m))


def solution(mesh):
    placed = (
        P(("region", "split"), None),
        P(("region", "split"), None, None, None),
        P(("region", "split"), None),
        P(("region", "split")),
        P("region", None, None),
        P(),
    )
    return jax.shard_map(
        functools.partial(local, (mesh.shape["region"], mesh.shape["split"])),
        mesh=mesh,
        in_specs=placed,
        out_specs=(P(("region", "split"), None), P()),
        check_vma=False,
    )
```

```python
import functools

import jax
import jax.numpy as jnp
from jax import lax
from jax.experimental import pallas as pl
from jax.experimental.pallas import tpu as pltpu
from jax.sharding import PartitionSpec as P

MESH = pl.DeviceIdType.MESH
HIGH = lax.Precision.HIGHEST
TRANSPOSED = (((1,), (1,)), ((), ()))
X = 4
PIECES = 3
AHEAD = 2
PANEL = 64
GROUP = 16
RS_AT, LINE_AT = ("select", 0), ("pass", 0)
SPREAD_AT = 2


def dot_high(a, b, dims=(((1,), (0,)), ((), ()))):
    return lax.dot_general(a, b, dims, precision=HIGH, preferred_element_type=jnp.float32)


def factor_inverse(block):
    size = block.shape[0]
    row_id = lax.broadcasted_iota(jnp.int32, (size, size), 0)
    same = row_id == lax.broadcasted_iota(jnp.int32, (size, size), 1)
    work = jnp.concatenate([block, jnp.where(same, 1.0, 0.0).astype(jnp.float32)], axis=1)
    rows = lax.broadcasted_iota(jnp.int32, work.shape, 0)
    for first in range(0, size, GROUP):
        wide = [
            jnp.broadcast_to(work[:, first + t : first + t + 1], work.shape) for t in range(GROUP)
        ]
        for t in range(GROUP):
            j = first + t
            over = 1.0 / wide[t][j : j + 1, :]
            below = jnp.where(rows > j, wide[t], 0.0)
            work = work - below * (work[j : j + 1, :] * over)
            for u in range(t + 1, GROUP):
                wide[u] = wide[u] - below * (wide[u][j : j + 1, :] * over)
    pivots = jnp.sum(jnp.where(same, work[:, :size], 0.0), axis=1, keepdims=True)
    return work[:, size:] * lax.rsqrt(pivots)


def kernel(dims, vec_hbm, hes_hbm, *refs):
    tables_hbm, (basis, inv_out, cross_out), scratch = refs[:4], refs[4:7], refs[7:]
    n_region, n_split, rb, bs, m, nnz, hb, total_rows = dims
    n_z, n_y = n_region // X, n_split // 2
    blocks = rb * n_split
    piece = bs // PIECES
    half_piece = piece // 2
    plane = X * n_split
    chunk = m // plane
    share = hb // 2

    it = iter(scratch)
    tables = [next(it) for _ in range(4)]
    cols, live, lists, bounds = tables
    vec, hes, hcat, picks = next(it), next(it), next(it), next(it)
    reg = [[next(it) for _ in range(PIECES)] for _ in range(3)]
    hal = [[next(it) for _ in range(PIECES)] for _ in range(3)]
    stg = [[next(it) for _ in range(PIECES)] for _ in range(3)]
    one, two, two_t, img = next(it), next(it), next(it), next(it)
    part = [next(it) for _ in range(2)]
    rs = [next(it) for _ in range(2)]
    zb = [next(it) for _ in range(2)]
    gram_full, own_chunk = next(it), [next(it) for _ in range(2)]
    full = [gram_full, cross_out]
    aug = next(it)
    in_sem, g_send, g_recv, h_send, h_recv, a_send, a_recv, token, out_sem = (
        next(it) for _ in range(9)
    )

    r = lax.axis_index("region")
    s = lax.axis_index("split")
    z, x = r // X, r % X
    y, c = s // 2, s % 2
    mate = y * 2 + 1 - c
    up_s = ((y + 1) % n_y) * 2 + c
    down_s = ((y + n_y - 1) % n_y) * 2 + c
    far_s = ((y + 2) % n_y) * 2 + c
    upper = (r + 1) % n_region
    lower = (r + n_region - 1) % n_region
    w = x * n_split + s

    copy_v = pltpu.make_async_copy(vec_hbm, vec, in_sem.at[0])
    copy_h = pltpu.make_async_copy(hes_hbm, hes, in_sem.at[1])
    copy_v.start()
    copies = [
        pltpu.make_async_copy(a, b, in_sem.at[2 + i])
        for i, (a, b) in enumerate(zip(tables_hbm, tables))
    ]
    for copy in copies:
        copy.start()
    copy_h.start()

    barrier = pltpu.get_barrier_semaphore()

    def signal(region, split):
        pl.semaphore_signal(barrier, inc=1, device_id=(region, split), device_id_type=MESH)

    def greet_split(o, carry):
        signal(r, (s + o) % n_split)
        return carry

    ring = (
        (z * X + (x + 1) % X, z * X + (x + X - 1) % X),
        (((z + 1) % n_z) * X + x, ((z + n_z - 1) % n_z) * X + x),
    )
    for region in (upper, lower) + ring[1] + ring[0]:
        signal(region, s)
    lax.fori_loop(1, n_split, greet_split, 0)

    rounds = (X // 2, max(n_z // 2 - 1, 0))
    ticks = []

    def pass_tokens(k):
        for axis in range(2):
            for side in range(2):
                if k <= rounds[axis]:
                    if k > 1:
                        pl.semaphore_wait(token.at[axis, k - 2, side], 1)
        for axis in range(2):
            for side in range(2):
                if k <= rounds[axis]:
                    pl.semaphore_signal(
                        token.at[axis, k - 1, side],
                        inc=1,
                        device_id=(ring[axis][side], s),
                        device_id_type=MESH,
                    )

    def tick():
        if len(ticks) < max(rounds):
            ticks.append(0)
            pass_tokens(len(ticks))

    def all_ticks():
        while len(ticks) < max(rounds):
            tick()
        for axis in range(2):
            for side in range(2):
                if rounds[axis] > 0:
                    pl.semaphore_wait(token.at[axis, rounds[axis] - 1, side], 1)

    def put_own(a, value):
        for q in range(PIECES):
            for b in range(rb):
                reg[a][q][s * rb + b] = value[b * bs + q * piece : b * bs + (q + 1) * piece, :].astype(
                    jnp.bfloat16
                )

    pending = []

    def remote(src, dst, ssem, rsem, region, split):
        copy = pltpu.make_async_remote_copy(
            src_ref=src,
            dst_ref=dst,
            send_sem=ssem,
            recv_sem=rsem,
            device_id=(region, split),
            device_id_type=MESH,
        )
        copy.start()
        pending.append(copy)
        return copy

    def gather_copy(a, q, kind, owner, rows, split):
        view = reg[a][q].at[pl.ds(owner * rb, rb), pl.ds(rows[0], rows[1] - rows[0]), :]
        at = (a * PIECES + q) * 9 + kind
        return remote(view, view, g_send.at[at], g_recv.at[at], r, split)

    whole, low, high = (0, piece), (0, half_piece), (half_piece, piece)

    def wait_gather(a, q, kind, owner, rows):
        view = reg[a][q].at[pl.ds(owner * rb, rb), pl.ds(rows[0], rows[1] - rows[0]), :]
        at = (a * PIECES + q) * 9 + kind
        pltpu.make_async_remote_copy(
            src_ref=view,
            dst_ref=view,
            send_sem=g_send.at[at],
            recv_sem=g_recv.at[at],
            device_id=(r, mate),
            device_id_type=MESH,
        ).wait_recv()

    def send_own(a, q):
        gather_copy(a, q, 0, s, whole, up_s)
        gather_copy(a, q, 1, s, whole, down_s)
        gather_copy(a, q, 4, s, whole, mate)

    def relay(a, q):
        wait_gather(a, q, 0, down_s, whole)
        gather_copy(a, q, 2, down_s, low, up_s)
        wait_gather(a, q, 1, up_s, whole)
        gather_copy(a, q, 3, up_s, high, down_s)
        gather_copy(a, q, 5, down_s, whole, mate)
        gather_copy(a, q, 6, up_s, whole, mate)

    def finish_gather(a, q):
        wait_gather(a, q, 2, far_s, low)
        gather_copy(a, q, 7, far_s, low, mate)
        wait_gather(a, q, 3, far_s, high)
        gather_copy(a, q, 8, far_s, high, mate)
        other = 1 - 2 * c
        wait_gather(a, q, 4, s + other, whole)
        wait_gather(a, q, 5, down_s + other, whole)
        wait_gather(a, q, 6, up_s + other, whole)
        wait_gather(a, q, 7, far_s + other, low)
        wait_gather(a, q, 8, far_s + other, high)

    def halo_view(a, q, d, core):
        return hal[a][q].at[pl.ds((1 - d) * hb + core * share, share)]

    def halo_copy(a, q, d, kind, src, dst, region, split):
        at = ((a * PIECES + q) * 2 + d) * 2 + kind
        return remote(src, dst, h_send.at[at], h_recv.at[at], region, split)

    def wait_halo(a, q, d, kind, core):
        view = halo_view(a, q, d, core)
        at = ((a * PIECES + q) * 2 + d) * 2 + kind
        pltpu.make_async_remote_copy(
            src_ref=view,
            dst_ref=view,
            send_sem=h_send.at[at],
            recv_sem=h_recv.at[at],
            device_id=(r, mate),
            device_id_type=MESH,
        ).wait_recv()

    def send_halo(a, q):
        for d in range(2):
            for j in range(share):
                stg[a][q][d, j] = reg[a][q][lists[0, d, c * share + j]]
            halo_copy(a, q, d, 0, stg[a][q].at[d], halo_view(a, q, d, c), (lower, upper)[d], s)

    def pass_halo(a, q):
        for d in (1, 0):
            wait_halo(a, q, d, 0, c)
            view = halo_view(a, q, d, c)
            halo_copy(a, q, d, 1, view, view, r, mate)

    def finish_halo(a, q):
        for d in (1, 0):
            wait_halo(a, q, d, 1, 1 - c)

    def start_apply(a):
        for q in range(min(AHEAD, PIECES)):
            send_own(a, q)

    def exchange(a, hooks=()):
        hooks = dict(hooks)

        def reached(name, q):
            if (name, q) in hooks:
                hooks[name, q]()

        for q in range(PIECES):
            relay(a, q)
            if q + AHEAD < PIECES:
                send_own(a, q + AHEAD)
            if a == 1:
                tick()
            reached("relay", q)
            if q >= 1:
                finish_gather(a, q - 1)
                send_halo(a, q - 1)
                reached("select", q - 1)
        finish_gather(a, PIECES - 1)
        send_halo(a, PIECES - 1)
        reached("select", PIECES - 1)
        tick()
        for q in range(PIECES):
            pass_halo(a, q)
            if a == 0:
                tick()
            reached("pass", q)
        for q in range(PIECES):
            finish_halo(a, q)

    def multiply(a, i):
        for k in range(nnz):
            col = cols[i, k]
            alive = k < live[i]
            inside = col < blocks
            near = jnp.where(inside, col, 0)
            away = jnp.where(alive, jnp.where(inside, 0, col - blocks), 2 * hb)
            use = jnp.logical_and(alive, inside)
            for q in range(PIECES):
                picks[pl.ds(k * bs + q * piece, piece), :] = jnp.where(
                    use, reg[a][q][near], hal[a][q][away]
                )
        return jnp.dot(hcat[i], picks[...], preferred_element_type=jnp.float32)

    def reduce_send(t):
        def body(o, carry):
            p = (w + o) % plane
            pltpu.make_async_remote_copy(
                src_ref=part[t].at[p],
                dst_ref=rs[t].at[o - 1],
                send_sem=a_send.at[t * 3],
                recv_sem=a_recv.at[t * 3],
                device_id=(z * X + p // n_split, p % n_split),
                device_id_type=MESH,
            ).start()
            return carry

        lax.fori_loop(plane // 2, plane, body, 0)
        lax.fori_loop(1, plane // 2, body, 0)

    def bulk(ref, at):
        return pltpu.make_async_remote_copy(
            src_ref=ref,
            dst_ref=ref,
            send_sem=a_send.at[at],
            recv_sem=a_recv.at[at],
            device_id=(r, mate),
            device_id_type=MESH,
        )

    def reduce_line(t):
        bulk(rs[t], t * 3).wait_recv()
        value = part[t][w]
        for o in range(plane - 1):
            value = value + rs[t][o]
        zb[t][z] = value

        def body(o, carry):
            pltpu.make_async_remote_copy(
                src_ref=zb[t].at[z],
                dst_ref=zb[t].at[z],
                send_sem=a_send.at[t * 3 + 1],
                recv_sem=a_recv.at[t * 3 + 1],
                device_id=(((z + n_z // 2 + (1 - 2 * (o % 2)) * ((o + 1) // 2)) % n_z) * X + x, s),
                device_id_type=MESH,
            ).start()
            return carry

        lax.fori_loop(0, n_z - 1, body, 0)

    def spread(t):
        bulk(zb[t].at[pl.ds(0, n_z - 1)], t * 3 + 1).wait_recv()
        value = zb[t][0]
        for o in range(1, n_z):
            value = value + zb[t][o]
        own_chunk[t][...] = value / total_rows
        pltpu.make_async_copy(own_chunk[t], full[t].at[w], out_sem.at[t]).start()

        def body(o, carry):
            p = (w + o) % plane
            pltpu.make_async_remote_copy(
                src_ref=own_chunk[t],
                dst_ref=full[t].at[w],
                send_sem=a_send.at[t * 3 + 2],
                recv_sem=a_recv.at[t * 3 + 2],
                device_id=(z * X + p // n_split, p % n_split),
                device_id_type=MESH,
            ).start()
            return carry

        lax.fori_loop(plane // 2, plane, body, 0)
        lax.fori_loop(1, plane // 2, body, 0)

    def collected(t):
        bulk(full[t].at[pl.ds(0, plane - 1)], t * 3 + 2).wait_recv()
        pltpu.make_async_copy(own_chunk[t], full[t].at[w], out_sem.at[t]).wait()

    def drain(t):
        bulk(rs[t], t * 3).wait_send()
        bulk(zb[t].at[pl.ds(0, n_z - 1)], t * 3 + 1).wait_send()
        bulk(full[t].at[pl.ds(0, plane - 1)], t * 3 + 2).wait_send()

    for a in range(3):
        for q in range(PIECES):
            hal[a][q][2 * hb] = jnp.zeros((piece, m), jnp.bfloat16)
    copy_v.wait()
    put_own(0, vec[...])
    pl.semaphore_wait(barrier, n_split - 1 + 6)
    start_apply(0)
    for copy in copies:
        copy.wait()
    copy_h.wait()

    def join(i, carry):
        for k in range(0, nnz, 2):
            hcat[i, :, k * bs : (k + 2) * bs] = jnp.concatenate([hes[i, k], hes[i, k + 1]], axis=1)
        return carry

    lax.fori_loop(0, rb, join, 0)
    exchange(0)
    centre = 0.5 * (bounds[0] + bounds[1])
    half = 0.5 * (bounds[1] - bounds[0])

    def step_one(i, carry):
        at = pl.ds(pl.multiple_of(i * bs, bs), bs)
        one[at, :] = (multiply(0, i) - centre * vec[at, :]) / half
        return carry

    def step_two(i, carry):
        at = pl.ds(pl.multiple_of(i * bs, bs), bs)
        two[at, :] = 2.0 * (multiply(1, i) - centre * one[at, :]) / half - vec[at, :]
        return carry

    def step_image(i, carry):
        at = pl.ds(pl.multiple_of(i * bs, bs), bs)
        img[at, :] = multiply(2, i)
        return carry

    lax.fori_loop(0, rb, step_one, 0)
    put_own(1, one[...])
    start_apply(1)
    exchange(1)
    lax.fori_loop(0, rb, step_two, 0)
    put_own(2, two[...])
    start_apply(2)
    two_t[...] = two[...].T
    part[0][...] = dot_high(two_t[...], two[...]).reshape(plane, chunk, m)
    all_ticks()
    exchange(
        2,
        {
            RS_AT: lambda: reduce_send(0),
            LINE_AT: lambda: reduce_line(0),
        },
    )
    lax.fori_loop(0, rb, step_image, 0)
    part[1][...] = dot_high(two_t[...], img[...]).reshape(plane, chunk, m)
    reduce_send(1)
    spread(0)
    reduce_line(1)

    row_id = lax.broadcasted_iota(jnp.int32, (m, m), 0)
    col_id = lax.broadcasted_iota(jnp.int32, (m, m), 1)
    aug[:, m:] = jnp.where(row_id == col_id, 1.0, 0.0).astype(jnp.float32)
    collected(0)
    aug[:, :m] = gram_full[...].reshape(m, m)

    def panel(p):
        at = p * PANEL
        end = at + PANEL
        inverse = factor_inverse(aug[at:end, at:end])
        rows = dot_high(inverse, aug[at:end, :])
        aug[at:end, :] = rows
        if end < m:
            left = rows[:, end:m].T
            aug[end:, :] = aug[end:, :] - dot_high(left, rows)

    panels = m // PANEL
    for p in range(panels):
        panel(p)
        if p == SPREAD_AT:
            spread(1)
    copy_inv = pltpu.make_async_copy(aug.at[:, pl.ds(m, m)], inv_out, out_sem.at[2])
    copy_inv.start()
    one[...] = dot_high(two[...], aug[:, m:], TRANSPOSED)
    copy_basis = pltpu.make_async_copy(one, basis, out_sem.at[3])
    copy_basis.start()
    for copy in pending:
        copy.wait_send()
    drain(0)
    drain(1)
    copy_inv.wait()
    copy_basis.wait()
    collected(1)


def finish(basis_in, inv_in, cross_in, basis_out, proj_out, basis, inv, cross, proj, sem):
    inputs = [
        pltpu.make_async_copy(a, b, sem.at[i])
        for i, (a, b) in enumerate(((inv_in, inv), (cross_in, cross), (basis_in, basis)))
    ]
    for copy in inputs:
        copy.start()
    inputs[0].wait()
    inputs[1].wait()
    proj[...] = dot_high(dot_high(inv[...], cross[...]), inv[...], TRANSPOSED)
    copy_proj = pltpu.make_async_copy(proj, proj_out, sem.at[3])
    copy_proj.start()
    inputs[2].wait()
    copy_basis = pltpu.make_async_copy(basis, basis_out, sem.at[4])
    copy_basis.start()
    copy_proj.wait()
    copy_basis.wait()


def local(sizes, vectors, hessian, block_cols, live_blocks, halo_lists, bounds):
    n_region, n_split = sizes
    rb, nnz, bs, _ = hessian.shape
    m = vectors.shape[1]
    hb = halo_lists.shape[2]
    rows = vectors.shape[0]
    dims = (n_region, n_split, rb, bs, m, nnz, hb, float(rows * n_region * n_split))
    piece = bs // PIECES
    blocks = rb * n_split
    plane = X * n_split
    chunk = m // plane
    n_z = n_region // X
    f32, bf16 = jnp.float32, jnp.bfloat16
    scratch = [pltpu.SMEM(a.shape, a.dtype) for a in (block_cols, live_blocks, halo_lists, bounds)]
    scratch += [
        pltpu.VMEM((rows, m), f32),
        pltpu.VMEM((rb, nnz, bs, bs), bf16),
        pltpu.VMEM((rb, bs, nnz * bs), bf16),
        pltpu.VMEM((nnz * bs, m), bf16),
    ]
    scratch += [pltpu.VMEM((blocks, piece, m), bf16) for _ in range(3 * PIECES)]
    scratch += [pltpu.VMEM((2 * hb + 1, piece, m), bf16) for _ in range(3 * PIECES)]
    scratch += [pltpu.VMEM((2, hb // 2, piece, m), bf16) for _ in range(3 * PIECES)]
    scratch += [
        pltpu.VMEM((rows, m), f32),
        pltpu.VMEM((rows, m), f32),
        pltpu.VMEM((m, rows), f32),
        pltpu.VMEM((rows, m), f32),
    ]
    scratch += [pltpu.VMEM((plane, chunk, m), f32)] * 2
    scratch += [pltpu.VMEM((plane - 1, chunk, m), f32)] * 2
    scratch += [pltpu.VMEM((n_z, chunk, m), f32)] * 2
    scratch += [pltpu.VMEM((plane, chunk, m), f32)]
    scratch += [pltpu.VMEM((chunk, m), f32)] * 2
    scratch += [pltpu.VMEM((m, 2 * m), f32)]
    dma = pltpu.SemaphoreType.DMA
    scratch += [
        dma((6,)),
        dma((27 * PIECES,)),
        dma((27 * PIECES,)),
        dma((12 * PIECES,)),
        dma((12 * PIECES,)),
        dma((6,)),
        dma((6,)),
        pltpu.SemaphoreType.REGULAR((2, 8, 2)),
        dma((4,)),
    ]
    hbm = pl.BlockSpec(memory_space=pl.ANY)
    basis, inverse, cross = pl.pallas_call(
        functools.partial(kernel, dims),
        out_shape=(
            jax.ShapeDtypeStruct((rows, m), f32),
            jax.ShapeDtypeStruct((m, m), f32),
            jax.ShapeDtypeStruct((plane, chunk, m), f32),
        ),
        in_specs=[hbm] * 6,
        out_specs=(hbm, hbm, hbm),
        scratch_shapes=scratch,
        compiler_params=pltpu.CompilerParams(
            collective_id=0, has_side_effects=True, vmem_limit_bytes=58 * 2**20
        ),
    )(vectors, hessian, block_cols, live_blocks, halo_lists, bounds)
    return pl.pallas_call(
        finish,
        out_shape=(jax.ShapeDtypeStruct((rows, m), f32), jax.ShapeDtypeStruct((m, m), f32)),
        in_specs=[hbm, hbm, hbm],
        out_specs=(hbm, hbm),
        scratch_shapes=[
            pltpu.VMEM((rows, m), f32),
            pltpu.VMEM((m, m), f32),
            pltpu.VMEM((m, m), f32),
            pltpu.VMEM((m, m), f32),
            dma((5,)),
        ],
        compiler_params=pltpu.CompilerParams(vmem_limit_bytes=58 * 2**20),
    )(basis, inverse, cross.reshape(m, m))


def solution(mesh):
    placed = (
        P(("region", "split"), None),
        P(("region", "split"), None, None, None),
        P(("region", "split"), None),
        P(("region", "split")),
        P("region", None, None),
        P(),
    )
    return jax.shard_map(
        functools.partial(local, (mesh.shape["region"], mesh.shape["split"])),
        mesh=mesh,
        in_specs=placed,
        out_specs=(P(("region", "split"), None), P()),
        check_vma=False,
    )
```
